32 devices in a mesh: bin: 4 (over z), row: 2 (over y), col: 4 (over x, core).
Axes of the slice: x: 2, y: 2, z: 4, core: 2. Of those that a mesh axis runs over, the one named last changes fastest.
Arguments:
- responses: bfloat16 [2, 4, 4096, 4096], P(None, 'bin', 'row', 'col'), may hold values from -6 to 6
- focusing: bfloat16 [2, 4, 16, 256, 256], P(None, 'bin', 'row'), may hold values from -0.25 to 0.25
- panel: bfloat16 [2, 4096, 256], P(None, 'col'), may hold values from -0.03125 to 0.03125
Outputs:
- projected: float32 [2, 256, 4096], P(None, 'col', 'row')
The draws below stay inside these ranges and needn't reach their ends.
All inputs are finite; a program needn't handle non-finite values.
Results may differ from the reference program's by a relative error of at most 0.0041.
Values may be sent and summed in bfloat16 or wider, within the bound.
No kernel may reach another device: no remote copies, remote signals or barrier semaphores. Data moves between devices by JAX's collectives and lax.ppermute only.
A program may use at most 128 MiB of HBM per device.

```python
import jax
import jax.numpy as jnp
from jax import lax

N = 4096
B = 256
K = 256
BINS = 4
NB = 16


def with_spikes(entries, stream_key, source, target, parts, factor):
    def block_of(dim):
        return (jnp.arange(entries.shape[dim]) // (entries.shape[dim] // parts)).reshape((-1,) + (1,) * (entries.ndim - 1 - dim))

    near = jax.random.permutation(stream_key, parts)[block_of(target)]
    second = (block_of(target) + parts // 2) % parts
    return jnp.where((block_of(source) == near) | (block_of(source) == second), factor * entries, entries)


def block_scale(key, shape, split, smallest, largest):
    loudness, own = 1.0, jax.random.fold_in(key, 6)
    for axis_at, parts in split:
        heights = jnp.exp(jax.random.uniform(jax.random.fold_in(own, axis_at), (parts,), jnp.float32, smallest / len(split), largest / len(split)))
        loudness = loudness * jnp.repeat(heights, shape[axis_at] // parts).reshape([-1 if axis == axis_at else 1 for axis in range(len(shape))])
    return loudness


def gaussian(key, extent, spread, limit, pieces=(), kind=jnp.bfloat16):
    entries = spread * jax.random.normal(key, extent, jnp.float32)
    if pieces:
        entries = entries * block_scale(key, extent, pieces, -0.22, 0.18)
    return jnp.clip(entries, -limit, limit).astype(kind)


def bell_draw_with(rng, dims, deviation, reach, shards, heavy, held_as=jnp.bfloat16):
    array = deviation * jax.random.normal(rng, dims, jnp.float32)
    if shards:
        array = array * block_scale(rng, dims, shards, -0.22, 0.18)
    return jnp.clip(with_spikes(array, jax.random.fold_in(rng, 3), *heavy), -reach, reach).astype(held_as)


def setup_inputs(seed: int = 0) -> dict:
    seeds = jax.random.split(jax.random.key(seed), 4)
    return {
        "responses": bell_draw_with(seeds[0], (2, BINS, N, N), 1.0, 6.0, ((1, 4), (2, 2), (3, 4)), (1, 3, 4, 2.0)),
        "focusing": gaussian(seeds[1], (2, BINS, NB, B, B), (2 * B) ** -0.5, 0.25, ((1, 4), (2, 2))),
        "panel": gaussian(seeds[2], (2, N, K), (2 * N * BINS) ** -0.5, 0.03125, ((1, 4),)),
    }


def settle(values):
    return values.astype(jnp.bfloat16)


def reference(responses, focusing, panel):
    pan_real = panel[0]
    pan_imag = panel[1]

    def one_bin(index, total):
        resp = lax.dynamic_index_in_dim(responses, index, 1, keepdims=False).astype(jnp.float32)
        blocks = lax.dynamic_index_in_dim(focusing, index, 1, keepdims=False).astype(jnp.float32)
        blk_real = blocks[0]
        blk_imag = blocks[1]
        resp_real = resp[0].reshape(NB, B, N)
        resp_imag = resp[1].reshape(NB, B, N)
        left_real = jnp.einsum("jab,jbm->jam", blk_real, resp_real) - jnp.einsum("jab,jbm->jam", blk_imag, resp_imag)
        left_imag = jnp.einsum("jab,jbm->jam", blk_real, resp_imag) + jnp.einsum("jab,jbm->jam", blk_imag, resp_real)
        left_real = settle(left_real).astype(jnp.float32).reshape(N, NB, B)
        left_imag = settle(left_imag).astype(jnp.float32).reshape(N, NB, B)
        foc_real = jnp.einsum("njb,jab->nja", left_real, blk_real) + jnp.einsum("njb,jab->nja", left_imag, blk_imag)
        foc_imag = jnp.einsum("njb,jab->nja", left_imag, blk_real) - jnp.einsum("njb,jab->nja", left_real, blk_imag)
        foc_real = settle(foc_real).reshape(N, N)
        foc_imag = settle(foc_imag).reshape(N, N)
        proj_real = jnp.dot(foc_real, pan_real, preferred_element_type=jnp.float32) - jnp.dot(foc_imag, pan_imag, preferred_element_type=jnp.float32)
        proj_imag = jnp.dot(foc_real, pan_imag, preferred_element_type=jnp.float32) + jnp.dot(foc_imag, pan_real, preferred_element_type=jnp.float32)
        return total + jnp.stack([proj_real.T, proj_imag.T])

    return lax.fori_loop(0, BINS, one_bin, jnp.zeros((2, K, N), jnp.float32))
```

```python
import functools

import jax
import jax.numpy as jnp
from jax import lax
from jax.experimental import pallas as pl
from jax.experimental.pallas import tpu as pltpu
from jax.sharding import PartitionSpec as P

CHUNKS = 4
BF16, F32 = jnp.bfloat16, jnp.float32


def mm(a, b, ca, cb):
    return lax.dot_general(a, b, (((ca,), (cb,)), ((), ())), preferred_element_type=F32)


def left_kernel(g_ref, r_ref, o_ref):
    g_re, g_im = g_ref[0, 0], g_ref[1, 0]
    r_re, r_im = r_ref[0], r_ref[1]
    o_ref[0] = (mm(g_re, r_re, 1, 0) - mm(g_im, r_im, 1, 0)).astype(BF16)
    o_ref[1] = (mm(g_re, r_im, 1, 0) + mm(g_im, r_re, 1, 0)).astype(BF16)


def left_focus(focusing, responses):
    _, blocks, size, _ = focusing.shape
    _, rows, cols = responses.shape
    return pl.pallas_call(
        left_kernel,
        grid=(blocks,),
        in_specs=[
            pl.BlockSpec((2, 1, size, size), lambda j: (0, j, 0, 0)),
            pl.BlockSpec((2, size, cols), lambda j: (0, j, 0)),
        ],
        out_specs=pl.BlockSpec((2, size, cols), lambda j: (0, j, 0)),
        out_shape=jax.ShapeDtypeStruct((2, rows, cols), BF16),
        cost_estimate=pl.CostEstimate(
            flops=8 * rows * size * cols, bytes_accessed=8 * rows * cols + 4 * rows * size, transcendentals=0
        ),
        name="left_focus",
    )(focusing, responses)


def slice_order(count):
    bits = count.bit_length() - 1
    return sorted(range(count), key=lambda e: tuple((e >> b) & 1 for b in range(bits)))


def weights_kernel(chunks, count, per_row, gathered, g_ref, p_ref, *rest):
    outs, scratch = rest[:chunks], rest[chunks]
    me = lax.axis_index("col")
    size = g_ref.shape[-1]
    cols = p_ref.shape[1]
    here = cols // size
    first = me * here if gathered else lax.rem(me * here, per_row)
    width = p_ref.shape[2]
    part = width // count
    piece = part // chunks
    for j in range(here):
        g_re, g_im = g_ref[0, first + j], g_ref[1, first + j]
        p_re, p_im = p_ref[0, pl.ds(j * size, size), :], p_ref[1, pl.ds(j * size, size), :]
        scratch[0] = mm(p_re, g_re, 0, 0) + mm(p_im, g_im, 0, 0)
        scratch[1] = mm(p_im, g_re, 0, 0) - mm(p_re, g_im, 0, 0)
        for at, e in enumerate(slice_order(count)):
            base = jnp.bitwise_xor(me, e) * part
            for i in range(chunks):
                for z in range(2):
                    start = pl.multiple_of(base + i * piece, piece)
                    outs[i][at, z, :, pl.ds(j * size, size)] = scratch[z, pl.ds(start, piece), :].astype(BF16)


def weights(focusing, panel, chunks, count, per_row, gathered):
    size = focusing.shape[-1]
    _, cols, width = panel.shape
    piece = width // count // chunks
    return pl.pallas_call(
        functools.partial(weights_kernel, chunks, count, per_row, gathered),
        out_shape=[jax.ShapeDtypeStruct((count, 2, piece, cols), BF16)] * chunks,
        scratch_shapes=[pltpu.VMEM((2, width, size), F32)],
        cost_estimate=pl.CostEstimate(
            flops=8 * cols * size * width, bytes_accessed=4 * cols * (2 * width + size), transcendentals=0
        ),
        name="weights",
    )(focusing, panel)


def product_kernel(own_row, own_ref, got_ref, left_ref, keep_ref, send_ref):
    count, _, piece, cols = own_ref.shape
    if own_row is None:
        h = own_ref[...]
    else:
        col = lax.axis_index("col")
        row = lax.axis_index("row")
        mine = row == (col * own_row[0]) // own_row[1]
        h = jnp.where(mine, own_ref[...], got_ref[...])
    h = h.reshape(count * 2 * piece, cols)
    tile = left_ref.shape[1]
    a = mm(h, left_ref[0], 1, 1).reshape(count, 2, piece, tile)
    b = mm(h, left_ref[1], 1, 1).reshape(count, 2, piece, tile)
    half = count // 2
    re, im = a[:, 0] - b[:, 1], a[:, 1] + b[:, 0]
    keep_ref[:, 0], keep_ref[:, 1] = re[:half], im[:half]
    send_ref[:, 0], send_ref[:, 1] = re[half:].astype(BF16), im[half:].astype(BF16)


def product(own, got, left, own_row):
    count, _, piece, cols = own.shape
    rows = left.shape[1]
    tile = min(512, rows)
    half = count // 2
    full = pl.BlockSpec(own.shape, lambda t: (0, 0, 0, 0))
    out = pl.BlockSpec((half, 2, piece, tile), lambda t: (0, 0, 0, t))
    return pl.pallas_call(
        functools.partial(product_kernel, own_row),
        grid=(rows // tile,),
        in_specs=[full, full, pl.BlockSpec((2, tile, cols), lambda t: (0, t, 0))],
        out_specs=[out, out],
        out_shape=[
            jax.ShapeDtypeStruct((half, 2, piece, rows), F32),
            jax.ShapeDtypeStruct((half, 2, piece, rows), BF16),
        ],
        cost_estimate=pl.CostEstimate(
            flops=8 * count * piece * cols * rows,
            bytes_accessed=4 * rows * cols + 12 * half * piece * rows,
            transcendentals=0,
        ),
        name="product",
    )(own, got, left)


def swap(value, axis, bit):
    count = lax.axis_size(axis)
    return lax.ppermute(value, axis, [(i, i ^ bit) for i in range(count)])


def reduce_chunk(keep, send):
    count = lax.axis_size("col")
    bit = 1
    while True:
        total = keep + swap(send, "col", bit).astype(F32)
        bit *= 2
        if bit == count:
            break
        half = total.shape[0] // 2
        keep, send = total[:half], total[half:].astype(BF16)
    total = total[0]
    bins = lax.axis_size("bin")
    bit = 1
    while bit < bins:
        kind = BF16 if bit * 4 >= bins else F32
        mine = total.astype(kind)
        total = mine.astype(F32) + swap(mine, "bin", bit).astype(F32)
        bit *= 2
    return total


def local(responses, focusing, panel):
    _, bins_here, tile_rows, tile_cols = responses.shape
    per_row, size = focusing.shape[2], focusing.shape[3]
    here = tile_cols // size
    count = lax.axis_size("col")
    row_count = lax.axis_size("row")
    gathered = not (row_count == 2 and per_row % here == 0)
    chunks = CHUNKS
    responses = responses.reshape(2, tile_rows, tile_cols)
    focusing = focusing.reshape(2, per_row, size, size)
    if gathered:
        blocks = lax.all_gather(focusing, "row", axis=1, tiled=True)
        own = weights(blocks, panel, chunks, count, per_row, True)
        got, own_row = own, None
    else:
        own = weights(focusing, panel, chunks, count, per_row, False)
        pairs = []
        for col in range(count):
            holder = (col * here) // per_row
            pairs.append((holder * count + col, (1 - holder) * count + col))
        got = [lax.ppermute(h, ("row", "col"), pairs) for h in own]
        own_row = (here, per_row)
    left = left_focus(focusing, responses)
    done = []
    for i in range(chunks):
        keep, send = product(own[i], got[i], left, own_row)
        done.append(reduce_chunk(keep, send))
    return jnp.concatenate(done, axis=1)


def solution(mesh):
    return jax.shard_map(
        local,
        mesh=mesh,
        in_specs=(
            P(None, "bin", "row", "col"),
            P(None, "bin", "row", None, None),
            P(None, "col", None),
        ),
        out_specs=P(None, "col", "row"),
        check_vma=False,
    )
```

```python
import functools

import jax
import jax.numpy as jnp
from jax import lax
from jax.experimental import pallas as pl
from jax.experimental.pallas import tpu as pltpu
from jax.sharding import PartitionSpec as P


SPLIT = (1, 1, 1, 1)
HALVED = (0, 1, 2, 3)
TILE = 512
BF16, F32 = jnp.bfloat16, jnp.float32
FIRST = F32


def mm(a, b, ca, cb):
    return lax.dot_general(a, b, (((ca,), (cb,)), ((), ())), preferred_element_type=F32)


VMEM = pl.BlockSpec(memory_space=pltpu.VMEM)
HBM = pl.BlockSpec(memory_space=pltpu.HBM)
SMALL = pltpu.CompilerParams(vmem_limit_bytes=8 * 2**20)
PARAMS = pltpu.CompilerParams(vmem_limit_bytes=20 * 2**20)


def in_vmem(value):
    return pltpu.with_memory_space_constraint(value, pltpu.VMEM)


def in_hbm(value):
    return pltpu.with_memory_space_constraint(value, pltpu.HBM)


def left_kernel(g_ref, first_ref, r_hbm, o_ref, second_ref, sem):
    blocks, size = g_ref.shape[1], g_ref.shape[2]
    head = first_ref.shape[1]
    copy = pltpu.make_async_copy(r_hbm.at[:, pl.ds(head, second_ref.shape[1]), :], second_ref, sem)
    copy.start()
    for j in range(blocks):
        if j * size == head:
            copy.wait()
        g_re, g_im = g_ref[0, j], g_ref[1, j]
        rows = pl.ds(j * size, size)
        src = first_ref if j * size < head else second_ref
        at = pl.ds(j * size if j * size < head else j * size - head, size)
        g = jnp.concatenate([jnp.concatenate([g_re, -g_im], 1), jnp.concatenate([g_im, g_re], 1)], 0)
        r = jnp.concatenate([src[0, at, :], src[1, at, :]], 0)
        y = mm(g, r, 1, 0)
        o_ref[0, :, rows] = y[:size].T.astype(BF16)
        o_ref[1, :, rows] = y[size:].T.astype(BF16)


def left_focus(focusing, first, responses):
    size = focusing.shape[2]
    _, rows, cols = responses.shape
    return pl.pallas_call(
        left_kernel,
        in_specs=[VMEM, VMEM, HBM],
        out_specs=VMEM,
        out_shape=pltpu.VMEM((2, cols, rows), BF16),
        scratch_shapes=[pltpu.VMEM((2, rows - first.shape[1], cols), BF16), pltpu.SemaphoreType.DMA(())],
        compiler_params=PARAMS,
        cost_estimate=pl.CostEstimate(
            flops=8 * rows * size * cols, bytes_accessed=8 * rows * cols + 4 * rows * size, transcendentals=0
        ),
        name="left_focus",
    )(focusing, first, in_hbm(responses))


def slice_order(count):
    bits = count.bit_length() - 1
    return sorted(range(count), key=lambda e: tuple((e >> b) & 1 for b in range(bits)))


def weights_kernel(pieces, count, per_row, gathered, g_hbm, p_hbm, f_hbm, r_hbm, *rest):
    chunks = len(pieces)
    outs = rest[:chunks]
    f_out, r_out, g_ref, p_ref, scratch, sems, extra = rest[chunks:]
    me = lax.axis_index("col")
    here, size = g_ref.shape[1], g_ref.shape[2]
    first = me * here if gathered else lax.rem(me * here, per_row)
    width = p_ref.shape[2]
    part = width // count
    copies = []
    for j in range(here):
        rows = pl.ds(j * size, size)
        copies.append(
            (
                pltpu.make_async_copy(g_hbm.at[:, first + j], g_ref.at[:, j], sems.at[0, j]),
                pltpu.make_async_copy(p_hbm.at[:, rows, :], p_ref.at[:, rows, :], sems.at[1, j]),
            )
        )
        for copy in copies[-1]:
            copy.start()
    later = (
        pltpu.make_async_copy(f_hbm, f_out, extra.at[0]),
        pltpu.make_async_copy(r_hbm.at[:, pl.ds(0, r_out.shape[1]), :], r_out, extra.at[1]),
    )
    for copy in later:
        copy.start()
    for j in range(here):
        for copy in copies[j]:
            copy.wait()
        rows = pl.ds(j * size, size)
        p_re, p_im = p_ref[0, rows, :], p_ref[1, rows, :]
        left = jnp.concatenate([jnp.concatenate([p_re, p_im], 1), jnp.concatenate([p_im, -p_re], 1)], 0)
        right = jnp.concatenate([g_ref[0, j], g_ref[1, j]], 0)
        scratch[...] = mm(left, right, 0, 0).reshape(2, width, size)
        for at, e in enumerate(slice_order(count)):
            base = jnp.bitwise_xor(me, e) * part
            done = 0
            for i, piece in enumerate(pieces):
                start = pl.multiple_of(base + done, 8)
                outs[i][at, :, :, rows] = scratch[:, pl.ds(start, piece), :].astype(BF16)
                done += piece
    for copy in later:
        copy.wait()


def weights(blocks, panel, focusing, responses, pieces, count, per_row, gathered):
    size = blocks.shape[-1]
    _, cols, width = panel.shape
    here = cols // size
    _, rows, wide = responses.shape
    head = (rows // size + 1) // 2 * size
    return pl.pallas_call(
        functools.partial(weights_kernel, pieces, count, per_row, gathered),
        in_specs=[HBM] * 4,
        out_specs=[VMEM] * (len(pieces) + 2),
        out_shape=[pltpu.VMEM((count, 2, piece, cols), BF16) for piece in pieces]
        + [pltpu.VMEM(focusing.shape, BF16), pltpu.VMEM((2, head, wide), BF16)],
        scratch_shapes=[
            pltpu.VMEM((2, here, size, size), BF16),
            pltpu.VMEM((2, cols, width), BF16),
            pltpu.VMEM((2, width, size), F32),
            pltpu.SemaphoreType.DMA((2, here)),
            pltpu.SemaphoreType.DMA((2,)),
        ],
        compiler_params=PARAMS,
        cost_estimate=pl.CostEstimate(
            flops=8 * cols * size * width, bytes_accessed=4 * cols * (2 * width + size), transcendentals=0
        ),
        name="weights",
    )(in_hbm(blocks), in_hbm(panel), in_hbm(focusing), in_hbm(responses))


def product_kernel(own_row, own_ref, got_ref, left_ref, keep_ref, send_ref, full_ref):
    count, _, piece, cols = own_ref.shape
    h = own_ref[...]
    if own_row is not None:
        mine = lax.axis_index("row") == (lax.axis_index("col") * own_row[0]) // own_row[1]
        h = jnp.where(mine, h, got_ref[...])
    full_ref[:, :, :, :cols] = h
    full_ref[:, 0, :, cols:] = -h[:, 1]
    full_ref[:, 1, :, cols:] = h[:, 0]
    rows = left_ref.shape[2]
    tile = min(TILE, rows)
    half = count // 2

    @pl.loop(0, rows // tile)
    def _(t):
        at = pl.ds(pl.multiple_of(t * tile, tile), tile)
        left = jnp.concatenate([left_ref[0, :, at], left_ref[1, :, at]], 0)
        out = mm(full_ref[...].reshape(count * 2 * piece, 2 * cols), left, 1, 0)
        out = out.reshape(count, 2, piece, tile)
        keep_ref[:, :, :, at] = out[:half]
        send_ref[:, :, :, at] = out[half:].astype(send_ref.dtype)


def product(own, got, left, own_row):
    count, _, piece, cols = own.shape
    rows = left.shape[2]
    half = count // 2
    return pl.pallas_call(
        functools.partial(product_kernel, own_row),
        in_specs=[VMEM] * 3,
        out_specs=[VMEM] * 2,
        out_shape=[pltpu.VMEM((half, 2, piece, rows), F32), pltpu.VMEM((half, 2, piece, rows), FIRST)],
        scratch_shapes=[pltpu.VMEM((count, 2, piece, 2 * cols), BF16)],
        compiler_params=PARAMS,
        cost_estimate=pl.CostEstimate(
            flops=8 * count * piece * cols * rows,
            bytes_accessed=4 * rows * cols + 12 * half * piece * rows,
            transcendentals=0,
        ),
        name="product",
    )(own, in_vmem(got), left)


def swap(value, axis, bit):
    count = lax.axis_size(axis)
    return lax.ppermute(value, axis, [(i, i ^ bit) for i in range(count)])


def small(kernel, outs, *args):
    size = sum(a.size for a in args)
    return pl.pallas_call(
        kernel,
        in_specs=[VMEM] * len(args),
        out_specs=[VMEM] * len(outs),
        out_shape=[pltpu.VMEM(shape, kind) for shape, kind in outs],
        compiler_params=SMALL,
        cost_estimate=pl.CostEstimate(flops=size, bytes_accessed=4 * size, transcendentals=0),
    )(*[in_vmem(a) for a in args])


def halve_kernel(keep_ref, got_ref, on_ref, send_ref):
    half = on_ref.shape[0]
    on_ref[...] = keep_ref[:half] + got_ref[:half].astype(F32)
    send_ref[...] = (keep_ref[half:] + got_ref[half:].astype(F32)).astype(send_ref.dtype)


def part_kernel(keep_ref, got_ref, on_ref, send_ref):
    mine = jnp.bitwise_and(lax.axis_index("bin"), 1)
    other = 1 - mine
    on_ref[...] = keep_ref[0, mine] + got_ref[0, mine].astype(F32)
    send_ref[...] = (keep_ref[0, other] + got_ref[0, other].astype(F32)).astype(send_ref.dtype)


def settle_kernel(keep_ref, got_ref, o_ref):
    o_ref[...] = (keep_ref[0] + got_ref[0].astype(F32)).astype(o_ref.dtype)


def add_kernel(a_ref, b_ref, o_ref):
    o_ref[...] = (a_ref[...].astype(F32) + b_ref[...].astype(F32)).astype(o_ref.dtype)


def reduce_chunk(i, keep, send):
    count, bins = lax.axis_size("col"), lax.axis_size("bin")
    bit = 1
    while True:
        got = swap(send, "col", bit)
        bit *= 2
        if bit == count:
            break
        shape = (keep.shape[0] // 2,) + keep.shape[1:]
        keep, send = small(halve_kernel, [(shape, F32), (shape, BF16)], keep, got)
    if i in HALVED:
        return sum_by_halves(keep, got, bins)
    mine, bit = None, 1
    while bit < bins:
        kind = BF16 if bit * 4 >= bins else F32
        if mine is None:
            (mine,) = small(settle_kernel, [(keep.shape[1:], kind)], keep, got)
        else:
            (mine,) = small(add_kernel, [(mine.shape, kind)], mine, got)
        got = swap(mine, "bin", bit)
        bit *= 2
    return mine, got


def sum_by_halves(keep, got, bins):
    shape = keep.shape[2:]
    half, send = small(part_kernel, [(shape, F32), (shape, BF16)], keep, got)
    got = swap(send, "bin", 1)
    bit = 2
    while bit < bins:
        (half,) = small(add_kernel, [(shape, BF16 if bit * 2 == bins else F32)], half, got)
        got = swap(half, "bin", bit)
        bit *= 2
    (half,) = small(add_kernel, [(shape, BF16)], half, got)
    return half, swap(half, "bin", 1)


def write_kernel(chunks, first, *refs):
    values, out, held, sem = refs[: 2 * len(chunks)], refs[-3], refs[-2], refs[-1]
    here = jnp.bitwise_and(lax.axis_index("bin"), 1)
    done = 0
    for k, i in enumerate(chunks):
        mine, other = values[2 * k], values[2 * k + 1]
        rows = pl.ds(done, mine.shape[-2])
        if i in HALVED:
            held[here, rows, :] = mine[...].astype(F32)
            held[1 - here, rows, :] = other[...].astype(F32)
        else:
            held[:, rows, :] = mine[...].astype(F32) + other[...].astype(F32)
        done += mine.shape[-2]
    copy = pltpu.make_async_copy(held, out.at[:, pl.ds(first, done), :], sem)
    copy.start()
    copy.wait()


def write(chunks, first, parts, shape, before):
    values = [in_vmem(v) for i in chunks for v in parts[i]]
    rows = sum(parts[i][0].shape[-2] for i in chunks)
    kept = [] if before is None else [before]
    return pl.pallas_call(
        functools.partial(write_kernel, chunks, first),
        in_specs=[VMEM] * len(values) + [HBM] * len(kept),
        out_specs=HBM,
        out_shape=jax.ShapeDtypeStruct(shape, F32),
        scratch_shapes=[pltpu.VMEM((2, rows, shape[2]), F32), pltpu.SemaphoreType.DMA(())],
        input_output_aliases={len(values): 0} if kept else {},
        compiler_params=SMALL,
        name="write",
    )(*values, *kept)


def split_of(part):
    return [part * s // sum(SPLIT) for s in SPLIT]


def local(responses, focusing, panel):
    _, _, tile_rows, tile_cols = responses.shape
    per_row, size = focusing.shape[2], focusing.shape[3]
    here = tile_cols // size
    count = lax.axis_size("col")
    row_count = lax.axis_size("row")
    gathered = not (row_count == 2 and per_row % here == 0)
    pieces = split_of(panel.shape[2] // count)
    chunks = len(pieces)
    responses = responses.reshape(2, tile_rows, tile_cols)
    focusing = focusing.reshape(2, per_row, size, size)
    if gathered:
        blocks = lax.all_gather(focusing, "row", axis=1, tiled=True)
        *own, g_in, r_in = weights(blocks, panel, focusing, responses, pieces, count, per_row, True)
        got, own_row = own, None
    else:
        *own, g_in, r_in = weights(focusing, panel, focusing, responses, pieces, count, per_row, False)
        pairs = []
        for col in range(count):
            holder = (col * here) // per_row
            pairs.append((holder * count + col, (1 - holder) * count + col))
        got = []
        for i in range(chunks):
            got.append(lax.ppermute(own[i], ("row", "col"), pairs))
        own_row = (here, per_row)
    left = left_focus(g_in, r_in, responses)
    parts = []
    for i in range(chunks):
        keep, send = product(own[i], got[i], left, own_row)
        parts.append(reduce_chunk(i, keep, send))
    shape = (2, sum(pieces), tile_rows)
    out, head = None, chunks - 1
    if head:
        out = write(tuple(range(head)), 0, parts, shape, None)
    return write((head,), sum(pieces[:head]), parts, shape, out)


def solution(mesh):
    return jax.shard_map(
        local,
        mesh=mesh,
        in_specs=(
            P(None, "bin", "row", "col"),
            P(None, "bin", "row", None, None),
            P(None, "col", None),
        ),
        out_specs=P(None, "col", "row"),
        check_vma=False,
    )
```

```python
import functools

import jax
import jax.numpy as jnp
from jax import lax
from jax.experimental import pallas as pl
from jax.experimental.pallas import tpu as pltpu
from jax.sharding import PartitionSpec as P


SPLIT = (1, 1, 1, 1)
PARTS = (1, 1, 1, 1)
HALVED = (0, 1, 2, 3)
TILE = 512
BF16, F32 = jnp.bfloat16, jnp.float32
FIRST = F32


def mm(a, b, ca, cb):
    return lax.dot_general(a, b, (((ca,), (cb,)), ((), ())), preferred_element_type=F32)


VMEM = pl.BlockSpec(memory_space=pltpu.VMEM)
HBM = pl.BlockSpec(memory_space=pltpu.HBM)
SMALL = pltpu.CompilerParams(vmem_limit_bytes=8 * 2**20)
PARAMS = pltpu.CompilerParams(vmem_limit_bytes=20 * 2**20)


def in_vmem(value):
    return pltpu.with_memory_space_constraint(value, pltpu.VMEM)


def in_hbm(value):
    return pltpu.with_memory_space_constraint(value, pltpu.HBM)


def left_kernel(g_ref, first_ref, r_hbm, o_ref, second_ref, sem):
    blocks, size = g_ref.shape[1], g_ref.shape[2]
    head = first_ref.shape[1]
    copy = pltpu.make_async_copy(r_hbm.at[:, pl.ds(head, second_ref.shape[1]), :], second_ref, sem)
    copy.start()
    for j in range(blocks):
        if j * size == head:
            copy.wait()
        g_re, g_im = g_ref[0, j], g_ref[1, j]
        rows = pl.ds(j * size, size)
        src = first_ref if j * size < head else second_ref
        at = pl.ds(j * size if j * size < head else j * size - head, size)
        g = jnp.concatenate([jnp.concatenate([g_re, -g_im], 1), jnp.concatenate([g_im, g_re], 1)], 0)
        r = jnp.concatenate([src[0, at, :], src[1, at, :]], 0)
        y = mm(g, r, 1, 0)
        o_ref[0, :, rows] = y[:size].T.astype(BF16)
        o_ref[1, :, rows] = y[size:].T.astype(BF16)


def left_focus(focusing, first, responses):
    size = focusing.shape[2]
    _, rows, cols = responses.shape
    return pl.pallas_call(
        left_kernel,
        in_specs=[VMEM, VMEM, HBM],
        out_specs=VMEM,
        out_shape=pltpu.VMEM((2, cols, rows), BF16),
        scratch_shapes=[pltpu.VMEM((2, rows - first.shape[1], cols), BF16), pltpu.SemaphoreType.DMA(())],
        compiler_params=PARAMS,
        cost_estimate=pl.CostEstimate(
            flops=8 * rows * size * cols, bytes_accessed=8 * rows * cols + 4 * rows * size, transcendentals=0
        ),
        name="left_focus",
    )(focusing, first, in_hbm(responses))


def slice_order(count):
    bits = count.bit_length() - 1
    return sorted(range(count), key=lambda e: tuple((e >> b) & 1 for b in range(bits)))


def weights_kernel(pieces, count, per_row, gathered, g_hbm, p_hbm, f_hbm, r_hbm, *rest):
    chunks = len(pieces)
    outs = rest[:chunks]
    f_out, r_out, g_ref, p_ref, scratch, sems, extra = rest[chunks:]
    me = lax.axis_index("col")
    here, size = g_ref.shape[1], g_ref.shape[2]
    first = me * here if gathered else lax.rem(me * here, per_row)
    width = p_ref.shape[2]
    part = width // count
    copies = []
    for j in range(here):
        rows = pl.ds(j * size, size)
        copies.append(
            (
                pltpu.make_async_copy(g_hbm.at[:, first + j], g_ref.at[:, j], sems.at[0, j]),
                pltpu.make_async_copy(p_hbm.at[:, rows, :], p_ref.at[:, rows, :], sems.at[1, j]),
            )
        )
        for copy in copies[-1]:
            copy.start()
    later = (
        pltpu.make_async_copy(f_hbm, f_out, extra.at[0]),
        pltpu.make_async_copy(r_hbm.at[:, pl.ds(0, r_out.shape[1]), :], r_out, extra.at[1]),
    )
    for copy in later:
        copy.start()
    for j in range(here):
        for copy in copies[j]:
            copy.wait()
        rows = pl.ds(j * size, size)
        p_re, p_im = p_ref[0, rows, :], p_ref[1, rows, :]
        left = jnp.concatenate([jnp.concatenate([p_re, p_im], 1), jnp.concatenate([p_im, -p_re], 1)], 0)
        right = jnp.concatenate([g_ref[0, j], g_ref[1, j]], 0)
        scratch[...] = mm(left, right, 0, 0).reshape(2, width, size)
        for at, e in enumerate(slice_order(count)):
            base = jnp.bitwise_xor(me, e) * part
            done = 0
            for i, piece in enumerate(pieces):
                start = pl.multiple_of(base + done, 8)
                outs[i][at, :, :, rows] = scratch[:, pl.ds(start, piece), :].astype(BF16)
                done += piece
    for copy in later:
        copy.wait()


def weights(blocks, panel, focusing, responses, pieces, count, per_row, gathered):
    size = blocks.shape[-1]
    _, cols, width = panel.shape
    here = cols // size
    _, rows, wide = responses.shape
    head = (rows // size + 1) // 2 * size
    return pl.pallas_call(
        functools.partial(weights_kernel, pieces, count, per_row, gathered),
        in_specs=[HBM] * 4,
        out_specs=[VMEM] * (len(pieces) + 2),
        out_shape=[pltpu.VMEM((count, 2, piece, cols), BF16) for piece in pieces]
        + [pltpu.VMEM(focusing.shape, BF16), pltpu.VMEM((2, head, wide), BF16)],
        scratch_shapes=[
            pltpu.VMEM((2, here, size, size), BF16),
            pltpu.VMEM((2, cols, width), BF16),
            pltpu.VMEM((2, width, size), F32),
            pltpu.SemaphoreType.DMA((2, here)),
            pltpu.SemaphoreType.DMA((2,)),
        ],
        compiler_params=PARAMS,
        cost_estimate=pl.CostEstimate(
            flops=8 * cols * size * width, bytes_accessed=4 * cols * (2 * width + size), transcendentals=0
        ),
        name="weights",
    )(in_hbm(blocks), in_hbm(panel), in_hbm(focusing), in_hbm(responses))


def product_kernel(own_row, parts, own_ref, got_ref, left_ref, *rest):
    outs, full_ref = rest[:-1], rest[-1]
    count, _, piece, cols = own_ref.shape
    h = own_ref[...]
    if own_row is not None:
        mine = lax.axis_index("row") == (lax.axis_index("col") * own_row[0]) // own_row[1]
        h = jnp.where(mine, h, got_ref[...])
    full_ref[:, :, :, :cols] = h
    full_ref[:, 0, :, cols:] = -h[:, 1]
    full_ref[:, 1, :, cols:] = h[:, 0]
    rows = left_ref.shape[2]
    tile = min(TILE, rows)
    half = count // 2

    @pl.loop(0, rows // tile)
    def _(t):
        at = pl.ds(pl.multiple_of(t * tile, tile), tile)
        left = jnp.concatenate([left_ref[0, :, at], left_ref[1, :, at]], 0)
        out = mm(full_ref[...].reshape(count * 2 * piece, 2 * cols), left, 1, 0)
        out = out.reshape(count, 2, piece, tile)
        size = piece // parts
        for k in range(parts):
            keep_ref, send_ref = outs[2 * k], outs[2 * k + 1]
            keep_ref[:, :, :, at] = out[:half, :, k * size : (k + 1) * size]
            send_ref[:, :, :, at] = out[half:, :, k * size : (k + 1) * size].astype(send_ref.dtype)


def product(own, got, left, own_row, parts):
    count, _, piece, cols = own.shape
    rows = left.shape[2]
    half = count // 2
    return pl.pallas_call(
        functools.partial(product_kernel, own_row, parts),
        in_specs=[VMEM] * 3,
        out_specs=[VMEM] * (2 * parts),
        out_shape=[pltpu.VMEM((half, 2, piece // parts, rows), kind) for kind in (F32, FIRST) * parts],
        scratch_shapes=[pltpu.VMEM((count, 2, piece, 2 * cols), BF16)],
        compiler_params=PARAMS,
        cost_estimate=pl.CostEstimate(
            flops=8 * count * piece * cols * rows,
            bytes_accessed=4 * rows * cols + 12 * half * piece * rows,
            transcendentals=0,
        ),
        name="product",
    )(own, in_vmem(got), left)


def swap(value, axis, bit):
    count = lax.axis_size(axis)
    return lax.ppermute(value, axis, [(i, i ^ bit) for i in range(count)])


def small(kernel, outs, *args):
    size = sum(a.size for a in args)
    return pl.pallas_call(
        kernel,
        in_specs=[VMEM] * len(args),
        out_specs=[VMEM] * len(outs),
        out_shape=[pltpu.VMEM(shape, kind) for shape, kind in outs],
        compiler_params=SMALL,
        cost_estimate=pl.CostEstimate(flops=size, bytes_accessed=4 * size, transcendentals=0),
    )(*[in_vmem(a) for a in args])


def halve_kernel(keep_ref, got_ref, on_ref, send_ref):
    half = on_ref.shape[0]
    on_ref[...] = keep_ref[:half] + got_ref[:half].astype(F32)
    send_ref[...] = (keep_ref[half:] + got_ref[half:].astype(F32)).astype(send_ref.dtype)


def part_kernel(keep_ref, got_ref, on_ref, send_ref):
    mine = jnp.bitwise_and(lax.axis_index("bin"), 1)
    other = 1 - mine
    on_ref[...] = keep_ref[0, mine] + got_ref[0, mine].astype(F32)
    send_ref[...] = (keep_ref[0, other] + got_ref[0, other].astype(F32)).astype(send_ref.dtype)


def settle_kernel(keep_ref, got_ref, o_ref):
    o_ref[...] = (keep_ref[0] + got_ref[0].astype(F32)).astype(o_ref.dtype)


def add_kernel(a_ref, b_ref, o_ref):
    o_ref[...] = (a_ref[...].astype(F32) + b_ref[...].astype(F32)).astype(o_ref.dtype)


def reduce_chunk(i, keep, send):
    count, bins = lax.axis_size("col"), lax.axis_size("bin")
    bit = 1
    while True:
        got = swap(send, "col", bit)
        bit *= 2
        if bit == count:
            break
        shape = (keep.shape[0] // 2,) + keep.shape[1:]
        keep, send = small(halve_kernel, [(shape, F32), (shape, BF16)], keep, got)
    if i in HALVED:
        return sum_by_halves(keep, got, bins)
    mine, bit = None, 1
    while bit < bins:
        kind = BF16 if bit * 4 >= bins else F32
        if mine is None:
            (mine,) = small(settle_kernel, [(keep.shape[1:], kind)], keep, got)
        else:
            (mine,) = small(add_kernel, [(mine.shape, kind)], mine, got)
        got = swap(mine, "bin", bit)
        bit *= 2
    return mine, got


def sum_by_halves(keep, got, bins):
    shape = keep.shape[2:]
    half, send = small(part_kernel, [(shape, F32), (shape, BF16)], keep, got)
    got = swap(send, "bin", 1)
    bit = 2
    while bit < bins:
        (half,) = small(add_kernel, [(shape, BF16 if bit * 2 == bins else F32)], half, got)
        got = swap(half, "bin", bit)
        bit *= 2
    (half,) = small(add_kernel, [(shape, BF16)], half, got)
    return half, swap(half, "bin", 1)


def write_kernel(chunks, first, *refs):
    values, out, held, sem = refs[: 2 * len(chunks)], refs[-3], refs[-2], refs[-1]
    here = jnp.bitwise_and(lax.axis_index("bin"), 1)
    done = 0
    for k, i in enumerate(chunks):
        mine, other = values[2 * k], values[2 * k + 1]
        rows = pl.ds(done, mine.shape[-2])
        if i in HALVED:
            held[here, rows, :] = mine[...].astype(F32)
            held[1 - here, rows, :] = other[...].astype(F32)
        else:
            held[:, rows, :] = mine[...].astype(F32) + other[...].astype(F32)
        done += mine.shape[-2]
    copy = pltpu.make_async_copy(held, out.at[:, pl.ds(first, done), :], sem)
    copy.start()
    copy.wait()


def write(chunks, first, parts, shape, before):
    values = [in_vmem(v) for i in chunks for v in parts[i]]
    rows = sum(parts[i][0].shape[-2] for i in chunks)
    kept = [] if before is None else [before]
    return pl.pallas_call(
        functools.partial(write_kernel, chunks, first),
        in_specs=[VMEM] * len(values) + [HBM] * len(kept),
        out_specs=HBM,
        out_shape=jax.ShapeDtypeStruct(shape, F32),
        scratch_shapes=[pltpu.VMEM((2, rows, shape[2]), F32), pltpu.SemaphoreType.DMA(())],
        input_output_aliases={len(values): 0} if kept else {},
        compiler_params=SMALL,
        name="write",
    )(*values, *kept)


def split_of(part):
    return [part * s // sum(SPLIT) for s in SPLIT]


def local(responses, focusing, panel):
    _, _, tile_rows, tile_cols = responses.shape
    per_row, size = focusing.shape[2], focusing.shape[3]
    here = tile_cols // size
    count = lax.axis_size("col")
    row_count = lax.axis_size("row")
    gathered = not (row_count == 2 and per_row % here == 0)
    pieces = split_of(panel.shape[2] // count)
    chunks = len(pieces)
    responses = responses.reshape(2, tile_rows, tile_cols)
    focusing = focusing.reshape(2, per_row, size, size)
    if gathered:
        blocks = lax.all_gather(focusing, "row", axis=1, tiled=True)
        *own, g_in, r_in = weights(blocks, panel, focusing, responses, pieces, count, per_row, True)
        got, own_row = own, None
    else:
        *own, g_in, r_in = weights(focusing, panel, focusing, responses, pieces, count, per_row, False)
        pairs = []
        for col in range(count):
            holder = (col * here) // per_row
            pairs.append((holder * count + col, (1 - holder) * count + col))
        got = []
        for i in range(chunks):
            got.append(lax.ppermute(own[i], ("row", "col"), pairs))
        own_row = (here, per_row)
    left = left_focus(g_in, r_in, responses)
    parts = []
    for i in range(chunks):
        made = product(own[i], got[i], left, own_row, PARTS[i])
        for k in range(PARTS[i]):
            parts.append(reduce_chunk(len(parts), made[2 * k], made[2 * k + 1]))
    shape = (2, sum(pieces), tile_rows)
    out, head = None, len(parts) - 1
    if head:
        out = write(tuple(range(head)), 0, parts, shape, None)
    return write((head,), shape[1] - parts[head][0].shape[-2], parts, shape, out)


def solution(mesh):
    return jax.shard_map(
        local,
        mesh=mesh,
        in_specs=(
            P(None, "bin", "row", "col"),
            P(None, "bin", "row", None, None),
            P(None, "col", None),
        ),
        out_specs=P(None, "col", "row"),
        check_vma=False,
    )
```

```python
import functools

import jax
import jax.numpy as jnp
from jax import lax
from jax.experimental import pallas as pl
from jax.experimental.pallas import tpu as pltpu
from jax.sharding import PartitionSpec as P


SPLIT = (1, 1, 1, 1)
PARTS = (1, 1, 1, 1)
HALVED = (0, 1, 2, 3)
TILE = 512
BF16, F32 = jnp.bfloat16, jnp.float32
FIRST = F32


def mm(a, b, ca, cb):
    return lax.dot_general(a, b, (((ca,), (cb,)), ((), ())), preferred_element_type=F32)


VMEM = pl.BlockSpec(memory_space=pltpu.VMEM)
HBM = pl.BlockSpec(memory_space=pltpu.HBM)
SMALL = pltpu.CompilerParams(vmem_limit_bytes=8 * 2**20)
PARAMS = pltpu.CompilerParams(vmem_limit_bytes=20 * 2**20)


def in_vmem(value):
    return pltpu.with_memory_space_constraint(value, pltpu.VMEM)


def in_hbm(value):
    return pltpu.with_memory_space_constraint(value, pltpu.HBM)


def left_kernel(g_ref, first_ref, r_hbm, o_ref, second_ref, sem):
    blocks, size = g_ref.shape[1], g_ref.shape[2]
    head = first_ref.shape[1]
    copy = pltpu.make_async_copy(r_hbm.at[:, pl.ds(head, second_ref.shape[1]), :], second_ref, sem)
    copy.start()
    for j in range(blocks):
        if j * size == head:
            copy.wait()
        g_re, g_im = g_ref[0, j], g_ref[1, j]
        rows = pl.ds(j * size, size)
        src = first_ref if j * size < head else second_ref
        at = pl.ds(j * size if j * size < head else j * size - head, size)
        g = jnp.concatenate([jnp.concatenate([g_re, -g_im], 1), jnp.concatenate([g_im, g_re], 1)], 0)
        r = jnp.concatenate([src[0, at, :], src[1, at, :]], 0)
        y = mm(g, r, 1, 0)
        o_ref[0, :, rows] = y[:size].T.astype(BF16)
        o_ref[1, :, rows] = y[size:].T.astype(BF16)


def left_focus(focusing, first, responses):
    size = focusing.shape[2]
    _, rows, cols = responses.shape
    return pl.pallas_call(
        left_kernel,
        in_specs=[VMEM, VMEM, HBM],
        out_specs=VMEM,
        out_shape=pltpu.VMEM((2, cols, rows), BF16),
        scratch_shapes=[pltpu.VMEM((2, rows - first.shape[1], cols), BF16), pltpu.SemaphoreType.DMA(())],
        compiler_params=PARAMS,
        cost_estimate=pl.CostEstimate(
            flops=8 * rows * size * cols, bytes_accessed=8 * rows * cols + 4 * rows * size, transcendentals=0
        ),
        name="left_focus",
    )(focusing, first, in_hbm(responses))


def slice_order(count):
    bits = count.bit_length() - 1
    return sorted(range(count), key=lambda e: tuple((e >> b) & 1 for b in range(bits)))


def weights_kernel(pieces, count, per_row, gathered, g_hbm, p_hbm, f_hbm, r_hbm, *rest):
    chunks = len(pieces)
    outs = rest[:chunks]
    f_out, r_out, g_ref, p_ref, scratch, sems, extra = rest[chunks:]
    me = lax.axis_index("col")
    here, size = g_ref.shape[1], g_ref.shape[2]
    first = me * here if gathered else lax.rem(me * here, per_row)
    width = p_ref.shape[2]
    part = width // count
    copies = []
    for j in range(here):
        rows = pl.ds(j * size, size)
        copies.append(
            (
                pltpu.make_async_copy(g_hbm.at[:, first + j], g_ref.at[:, j], sems.at[0, j]),
                pltpu.make_async_copy(p_hbm.at[:, rows, :], p_ref.at[:, rows, :], sems.at[1, j]),
            )
        )
        for copy in copies[-1]:
            copy.start()
    later = (
        pltpu.make_async_copy(f_hbm, f_out, extra.at[0]),
        pltpu.make_async_copy(r_hbm.at[:, pl.ds(0, r_out.shape[1]), :], r_out, extra.at[1]),
    )
    for copy in later:
        copy.start()
    for j in range(here):
        for copy in copies[j]:
            copy.wait()
        rows = pl.ds(j * size, size)
        p_re, p_im = p_ref[0, rows, :], p_ref[1, rows, :]
        left = jnp.concatenate([jnp.concatenate([p_re, p_im], 1), jnp.concatenate([p_im, -p_re], 1)], 0)
        right = jnp.concatenate([g_ref[0, j], g_ref[1, j]], 0)
        scratch[...] = mm(left, right, 0, 0).reshape(2, width, size)
        for at, e in enumerate(slice_order(count)):
            base = jnp.bitwise_xor(me, e) * part
            done = 0
            for i, piece in enumerate(pieces):
                start = pl.multiple_of(base + done, 8)
                outs[i][at, :, :, rows] = scratch[:, pl.ds(start, piece), :].astype(BF16)
                done += piece
    for copy in later:
        copy.wait()


def weights(blocks, panel, focusing, responses, pieces, count, per_row, gathered):
    size = blocks.shape[-1]
    _, cols, width = panel.shape
    here = cols // size
    _, rows, wide = responses.shape
    head = (rows // size + 1) // 2 * size
    return pl.pallas_call(
        functools.partial(weights_kernel, pieces, count, per_row, gathered),
        in_specs=[HBM] * 4,
        out_specs=[VMEM] * (len(pieces) + 2),
        out_shape=[pltpu.VMEM((count, 2, piece, cols), BF16) for piece in pieces]
        + [pltpu.VMEM(focusing.shape, BF16), pltpu.VMEM((2, head, wide), BF16)],
        scratch_shapes=[
            pltpu.VMEM((2, here, size, size), BF16),
            pltpu.VMEM((2, cols, width), BF16),
            pltpu.VMEM((2, width, size), F32),
            pltpu.SemaphoreType.DMA((2, here)),
            pltpu.SemaphoreType.DMA((2,)),
        ],
        compiler_params=PARAMS,
        cost_estimate=pl.CostEstimate(
            flops=8 * cols * size * width, bytes_accessed=4 * cols * (2 * width + size), transcendentals=0
        ),
        name="weights",
    )(in_hbm(blocks), in_hbm(panel), in_hbm(focusing), in_hbm(responses))


def product_kernel(own_row, parts, own_ref, got_ref, left_ref, *rest):
    outs, full_ref = rest[:-1], rest[-1]
    count, _, piece, cols = own_ref.shape
    h = own_ref[...]
    if own_row is not None:
        mine = lax.axis_index("row") == (lax.axis_index("col") * own_row[0]) // own_row[1]
        h = jnp.where(mine, h, got_ref[...])
    full_ref[:, :, :, :cols] = h
    full_ref[:, 0, :, cols:] = -h[:, 1]
    full_ref[:, 1, :, cols:] = h[:, 0]
    rows = left_ref.shape[2]
    tile = min(TILE, rows)
    half = count // 2

    @pl.loop(0, rows // tile)
    def _(t):
        at = pl.ds(pl.multiple_of(t * tile, tile), tile)
        left = jnp.concatenate([left_ref[0, :, at], left_ref[1, :, at]], 0)
        out = mm(full_ref[...].reshape(count * 2 * piece, 2 * cols), left, 1, 0)
        out = out.reshape(count, 2, piece, tile)
        size = piece // parts
        for k in range(parts):
            keep_ref, send_ref = outs[2 * k], outs[2 * k + 1]
            keep_ref[:, :, :, at] = out[:half, :, k * size : (k + 1) * size]
            send_ref[:, :, :, at] = out[half:, :, k * size : (k + 1) * size].astype(send_ref.dtype)


def product(own, got, left, own_row, parts):
    count, _, piece, cols = own.shape
    rows = left.shape[2]
    half = count // 2
    return pl.pallas_call(
        functools.partial(product_kernel, own_row, parts),
        in_specs=[VMEM] * 3,
        out_specs=[VMEM] * (2 * parts),
        out_shape=[pltpu.VMEM((half, 2, piece // parts, rows), kind) for kind in (F32, FIRST) * parts],
        scratch_shapes=[pltpu.VMEM((count, 2, piece, 2 * cols), BF16)],
        compiler_params=PARAMS,
        cost_estimate=pl.CostEstimate(
            flops=8 * count * piece * cols * rows,
            bytes_accessed=4 * rows * cols + 12 * half * piece * rows,
            transcendentals=0,
        ),
        name="product",
    )(own, in_vmem(got), left)


def swap(value, axis, bit):
    count = lax.axis_size(axis)
    return lax.ppermute(value, axis, [(i, i ^ bit) for i in range(count)])


def small(kernel, outs, *args):
    size = sum(a.size for a in args)
    return pl.pallas_call(
        kernel,
        in_specs=[VMEM] * len(args),
        out_specs=[VMEM] * len(outs),
        out_shape=[pltpu.VMEM(shape, kind) for shape, kind in outs],
        compiler_params=SMALL,
        cost_estimate=pl.CostEstimate(flops=size, bytes_accessed=4 * size, transcendentals=0),
    )(*[in_vmem(a) for a in args])


def halve_kernel(keep_ref, got_ref, on_ref, send_ref):
    half = on_ref.shape[0]
    on_ref[...] = keep_ref[:half] + got_ref[:half].astype(F32)
    send_ref[...] = (keep_ref[half:] + got_ref[half:].astype(F32)).astype(send_ref.dtype)


def part_kernel(keep_ref, got_ref, on_ref, send_ref):
    mine = jnp.bitwise_and(lax.axis_index("bin"), 1)
    other = 1 - mine
    on_ref[...] = keep_ref[0, mine] + got_ref[0, mine].astype(F32)
    send_ref[...] = (keep_ref[0, other] + got_ref[0, other].astype(F32)).astype(send_ref.dtype)


def settle_kernel(keep_ref, got_ref, o_ref):
    o_ref[...] = (keep_ref[0] + got_ref[0].astype(F32)).astype(o_ref.dtype)


def add_kernel(a_ref, b_ref, o_ref):
    o_ref[...] = (a_ref[...].astype(F32) + b_ref[...].astype(F32)).astype(o_ref.dtype)


def reduce_chunk(i, keep, send):
    count, bins = lax.axis_size("col"), lax.axis_size("bin")
    bit = 1
    while True:
        got = swap(send, "col", bit)
        bit *= 2
        if bit == count:
            break
        shape = (keep.shape[0] // 2,) + keep.shape[1:]
        keep, send = small(halve_kernel, [(shape, F32), (shape, BF16)], keep, got)
    if i in HALVED:
        return sum_by_halves(keep, got, bins)
    mine, bit = None, 1
    while bit < bins:
        kind = BF16 if bit * 4 >= bins else F32
        if mine is None:
            (mine,) = small(settle_kernel, [(keep.shape[1:], kind)], keep, got)
        else:
            (mine,) = small(add_kernel, [(mine.shape, kind)], mine, got)
        got = swap(mine, "bin", bit)
        bit *= 2
    return mine, got


def sum_by_halves(keep, got, bins):
    shape = keep.shape[2:]
    half, send = small(part_kernel, [(shape, F32), (shape, BF16)], keep, got)
    got = swap(send, "bin", 1)
    bit = 2
    while bit < bins:
        (half,) = small(add_kernel, [(shape, BF16 if bit * 2 == bins else F32)], half, got)
        got = swap(half, "bin", bit)
        bit *= 2
    (half,) = small(add_kernel, [(shape, BF16)], half, got)
    return half, swap(half, "bin", 1)


def write_kernel(chunks, first, *refs):
    values, out, held, sem = refs[: 2 * len(chunks)], refs[-3], refs[-2], refs[-1]
    here = jnp.bitwise_and(lax.axis_index("bin"), 1)
    done = 0
    for k, i in enumerate(chunks):
        mine, other = values[2 * k], values[2 * k + 1]
        rows = pl.ds(done, mine.shape[-2])
        if i in HALVED:
            held[here, rows, :] = mine[...].astype(F32)
            held[1 - here, rows, :] = other[...].astype(F32)
        else:
            held[:, rows, :] = mine[...].astype(F32) + other[...].astype(F32)
        done += mine.shape[-2]
    copy = pltpu.make_async_copy(held, out.at[:, pl.ds(first, done), :], sem)
    copy.start()
    copy.wait()


def write(chunks, first, parts, shape, before):
    values = [in_vmem(v) for i in chunks for v in parts[i]]
    rows = sum(parts[i][0].shape[-2] for i in chunks)
    kept = [] if before is None else [before]
    return pl.pallas_call(
        functools.partial(write_kernel, chunks, first),
        in_specs=[VMEM] * len(values) + [HBM] * len(kept),
        out_specs=HBM,
        out_shape=jax.ShapeDtypeStruct(shape, F32),
        scratch_shapes=[pltpu.VMEM((2, rows, shape[2]), F32), pltpu.SemaphoreType.DMA(())],
        input_output_aliases={len(values): 0} if kept else {},
        compiler_params=SMALL,
        name="write",
    )(*values, *kept)


def split_of(part):
    return [part * s // sum(SPLIT) for s in SPLIT]


def local(responses, focusing, panel):
    _, _, tile_rows, tile_cols = responses.shape
    per_row, size = focusing.shape[2], focusing.shape[3]
    here = tile_cols // size
    count = lax.axis_size("col")
    row_count = lax.axis_size("row")
    gathered = not (row_count == 2 and per_row % here == 0)
    pieces = split_of(panel.shape[2] // count)
    chunks = len(pieces)
    responses = responses.reshape(2, tile_rows, tile_cols)
    focusing = focusing.reshape(2, per_row, size, size)
    if gathered:
        blocks = lax.all_gather(focusing, "row", axis=1, tiled=True)
        *own, g_in, r_in = weights(blocks, panel, focusing, responses, pieces, count, per_row, True)
        got, own_row = own, None
    else:
        *own, g_in, r_in = weights(focusing, panel, focusing, responses, pieces, count, per_row, False)
        pairs = []
        for col in range(count):
            holder = (col * here) // per_row
            pairs.append((holder * count + col, (1 - holder) * count + col))
        got = []
        for i in range(chunks):
            got.append(lax.ppermute(own[i], ("row", "col"), pairs))
        own_row = (here, per_row)
    left = left_focus(g_in, r_in, responses)
    parts = []
    for i in range(chunks):
        made = product(own[i], got[i], left, own_row, PARTS[i])
        for k in range(PARTS[i]):
            parts.append(reduce_chunk(len(parts), made[2 * k], made[2 * k + 1]))
    shape = (2, sum(pieces), tile_rows)
    out, head = None, len(parts) // 2
    if head:
        out = write(tuple(range(head)), 0, parts, shape, None)
    first = sum(part[0].shape[-2] for part in parts[:head])
    return write(tuple(range(head, len(parts))), first, parts, shape, out)


def solution(mesh):
    return jax.shard_map(
        local,
        mesh=mesh,
        in_specs=(
            P(None, "bin", "row", "col"),
            P(None, "bin", "row", None, None),
            P(None, "col", None),
        ),
        out_specs=P(None, "col", "row"),
        check_vma=False,
    )
```
